32 devices in a mesh: cube: 8 (over z, y), blk: 4 (over x, core).
Axes of the slice: x: 2, y: 2, z: 4, core: 2. Of those that a mesh axis runs over, the one named last changes fastest.
Arguments:
- rhs_root: bfloat16 [1, 10240, 128], P(None, 'blk'), may hold values from -6 to 6
- rhs_mid: bfloat16 [2, 10240, 128], P(None, 'blk'), may hold values from -6 to 6
- rhs_leaf: bfloat16 [4, 10240, 128], P(None, 'blk'), may hold values from -6 to 6
- pivot_root: bfloat16 [2, 10240, 10240], P(None, 'cube', 'blk'), may hold values from -0.0625 to 0.0625
- pivot_mid: bfloat16 [2, 20480, 10240], P(None, 'cube', 'blk'), may hold values from -0.0625 to 0.0625
- pivot_leaf: bfloat16 [2, 40960, 10240], P(None, 'cube', 'blk'), may hold values from -0.0625 to 0.0625
- coupling_mid: bfloat16 [2, 2560, 10240], P(None, 'cube', 'blk'), may hold values from -0.0625 to 0.0625
- coupling_leaf: bfloat16 [2, 5120, 10240], P(None, 'cube', 'blk'), may hold values from -0.0625 to 0.0625
- front_blocks: int32 [7], replicated, may hold values from 40 to 80, as said below
- child_map: int32 [6, 10], replicated, may hold values from 0 to 79
Outputs:
- solution_root: bfloat16 [4, 2560, 128], P('blk', 'cube')
- solution_mid: bfloat16 [4, 5120, 128], P('blk', 'cube')
- solution_leaf: bfloat16 [4, 10240, 128], P('blk', 'cube')
The draws below stay inside these ranges and needn't reach their ends.
Inputs may be any that keep to these rules, and one draw needn't show every extreme that they name: `front_blocks`: entry 0 is the root, entries 1 and 2 the level-1 fronts, 3 to 6 the level-2 fronts; at least one front is full in every draw. `child_map`: rows 0 and 1 belong to the level-1 fronts, row 2 + q to level-2 front q; targets may repeat within and across children.
All inputs are finite; a program needn't handle non-finite values.
Results may differ from the reference program's by a relative error of at most 0.013.
Values may be sent and summed in bfloat16 or wider, within the bound.
A program may use at most 192 MiB of HBM per device.

```python
import jax
import jax.numpy as jnp

SEPARATOR = 10240
UPDATES = 1280
BLOCK_ROWS = 128
SOURCES = 64
N_BLK = 4


def draw_front_blocks(key, part):
    first, second = jax.random.split(key)
    largest = SEPARATOR // BLOCK_ROWS
    values = jax.random.randint(first, (7,), largest // 2, largest + 1)
    chosen = jax.random.randint(second, (), 0, 7)
    return jnp.where(jnp.arange(7) == chosen, largest, values).astype(jnp.int32)


def place_ends(array, own_key, smallest, high):
    extent = array.shape
    spot = [jax.random.randint(jax.random.fold_in(own_key, axis), (), 0, extent[axis]) for axis in range(len(extent))]
    array = array.at[tuple(spot)].set(smallest)
    longest = extent.index(max(extent))
    spot[longest] = (spot[longest] + 1) % extent[longest]
    return array.at[tuple(spot)].set(high)


def levels(stream_key, extent, cuts, low, top_value):
    def one(dim, shards_of):
        heights = jax.random.uniform(jax.random.fold_in(jax.random.fold_in(stream_key, 6), dim), (shards_of,), jnp.float32, low / len(cuts), top_value / len(cuts))
        return jnp.repeat(jnp.exp(heights), extent[dim] // shards_of).reshape((-1,) + (1,) * (len(extent) - dim - 1))

    factor_of = one(*cuts[0])
    for cut in cuts[1:]:
        factor_of = factor_of * one(*cut)
    return factor_of


def normal_values(rng, dims, spread, bound, cuts=(), held_as=jnp.bfloat16):
    result = spread * jax.random.normal(rng, dims, jnp.float32)
    if cuts:
        result = result * levels(rng, dims, cuts, -0.22, 0.18)
    return jnp.clip(result, -bound, bound).astype(held_as)


def setup_inputs(seed: int = 0) -> dict:
    keys = jax.random.split(jax.random.key(seed), 11)
    rhs_root = normal_values(keys[0], (1, SEPARATOR, 2 * SOURCES), 1.0, 6.0, ((1, 4),))
    rhs_mid = normal_values(keys[1], (2, SEPARATOR, 2 * SOURCES), 1.0, 6.0, ((1, 4),))
    rhs_leaf = normal_values(keys[2], (4, SEPARATOR, 2 * SOURCES), 1.0, 6.0, ((1, 4),))
    pivot_root = normal_values(keys[3], (2, SEPARATOR, SEPARATOR), SEPARATOR ** -0.5, 0.0625, ((1, 8), (2, 4)))
    pivot_mid = normal_values(keys[4], (2, 2 * SEPARATOR, SEPARATOR), SEPARATOR ** -0.5, 0.0625, ((1, 8), (2, 4)))
    pivot_leaf = normal_values(keys[5], (2, 4 * SEPARATOR, SEPARATOR), SEPARATOR ** -0.5, 0.0625, ((1, 8), (2, 4)))
    coupling_mid = normal_values(keys[6], (2, 2 * UPDATES, SEPARATOR), SEPARATOR ** -0.5, 0.0625, ((1, 8), (2, 4)))
    coupling_leaf = normal_values(keys[7], (2, 4 * UPDATES, SEPARATOR), SEPARATOR ** -0.5, 0.0625, ((1, 8), (2, 4)))
    front_blocks = draw_front_blocks(jax.random.fold_in(keys[10], 71), 0)
    child_map = place_ends(jax.random.randint(keys[9], (6, UPDATES // BLOCK_ROWS), 0, SEPARATOR // BLOCK_ROWS), jax.random.fold_in(keys[9], 1), 0, (SEPARATOR // BLOCK_ROWS) - 1).astype(jnp.int32)
    return dict(rhs_root=rhs_root, rhs_mid=rhs_mid, rhs_leaf=rhs_leaf, pivot_root=pivot_root, pivot_mid=pivot_mid, pivot_leaf=pivot_leaf, coupling_mid=coupling_mid, coupling_leaf=coupling_leaf, front_blocks=front_blocks, child_map=child_map)


def rotate_parts(vec):
    half = vec.shape[1] // 2
    return jnp.concatenate([-vec[:, half:], vec[:, :half]], axis=1)


def complex_apply(matrix, vec):
    first = jnp.dot(matrix[0], vec, preferred_element_type=jnp.float32)
    second = jnp.dot(matrix[1], rotate_parts(vec), preferred_element_type=jnp.float32)
    return first + second


def complex_apply_t(matrix, vec):
    first = jnp.dot(matrix[0].T, vec, preferred_element_type=jnp.float32)
    second = jnp.dot(matrix[1].T, rotate_parts(vec), preferred_element_type=jnp.float32)
    return first + second


def target_rows(targets):
    offsets = jnp.arange(BLOCK_ROWS, dtype=jnp.int32)
    return (targets[:, None].astype(jnp.int32) * BLOCK_ROWS + offsets[None, :]).reshape(-1)


def spread_update(update, targets):
    empty = jnp.zeros((SEPARATOR, 2 * SOURCES), jnp.float32)
    return empty.at[target_rows(targets)].add(update.astype(jnp.float32))


def mask_of(front_blocks, index):
    rows = jnp.arange(SEPARATOR, dtype=jnp.int32)
    return (rows < front_blocks[index] * BLOCK_ROWS).astype(jnp.float32)[:, None]


def forward_front(pivot, coupling, gathered, mask):
    masked = (mask * gathered).astype(jnp.bfloat16)
    solved = (mask * complex_apply(pivot, masked)).astype(jnp.bfloat16)
    update = None
    if coupling is not None:
        update = complex_apply(coupling, masked).astype(jnp.bfloat16)
    return solved, update


def layout(fronts):
    stacked = jnp.stack(fronts)
    count = stacked.shape[0]
    shaped = stacked.reshape(count, N_BLK, SEPARATOR // N_BLK, 2 * SOURCES)
    return shaped.transpose(1, 0, 2, 3).reshape(N_BLK, count * SEPARATOR // N_BLK, 2 * SOURCES)


def reference(rhs_root, rhs_mid, rhs_leaf, pivot_root, pivot_mid, pivot_leaf, coupling_mid, coupling_leaf, front_blocks, child_map):
    sep = SEPARATOR
    upd = UPDATES
    solved_leaf, update_leaf = [], []
    for front in range(4):
        pivot = pivot_leaf[:, front * sep:(front + 1) * sep, :]
        coupling = coupling_leaf[:, front * upd:(front + 1) * upd, :]
        gathered = rhs_leaf[front].astype(jnp.float32)
        solved, update = forward_front(pivot, coupling, gathered, mask_of(front_blocks, 3 + front))
        solved_leaf.append(solved)
        update_leaf.append(update)
    solved_mid, update_mid = [], []
    for front in range(2):
        pivot = pivot_mid[:, front * sep:(front + 1) * sep, :]
        coupling = coupling_mid[:, front * upd:(front + 1) * upd, :]
        gathered = rhs_mid[front].astype(jnp.float32)
        gathered = gathered - spread_update(update_leaf[2 * front], child_map[2 + 2 * front])
        gathered = gathered - spread_update(update_leaf[2 * front + 1], child_map[3 + 2 * front])
        solved, update = forward_front(pivot, coupling, gathered, mask_of(front_blocks, 1 + front))
        solved_mid.append(solved)
        update_mid.append(update)
    gathered = rhs_root[0].astype(jnp.float32)
    gathered = gathered - spread_update(update_mid[0], child_map[0]) - spread_update(update_mid[1], child_map[1])
    mask_root = mask_of(front_blocks, 0)
    solved_root, unused = forward_front(pivot_root, None, gathered, mask_root)
    answer_root = (mask_root * complex_apply_t(pivot_root, solved_root)).astype(jnp.bfloat16)
    answer_mid = []
    for front in range(2):
        pivot = pivot_mid[:, front * sep:(front + 1) * sep, :]
        coupling = coupling_mid[:, front * upd:(front + 1) * upd, :]
        pulled = answer_root[target_rows(child_map[front])]
        term = complex_apply_t(pivot, solved_mid[front]) - complex_apply_t(coupling, pulled)
        answer_mid.append((mask_of(front_blocks, 1 + front) * term).astype(jnp.bfloat16))
    answer_leaf = []
    for front in range(4):
        pivot = pivot_leaf[:, front * sep:(front + 1) * sep, :]
        coupling = coupling_leaf[:, front * upd:(front + 1) * upd, :]
        pulled = answer_mid[front // 2][target_rows(child_map[2 + front])]
        term = complex_apply_t(pivot, solved_leaf[front]) - complex_apply_t(coupling, pulled)
        answer_leaf.append((mask_of(front_blocks, 3 + front) * term).astype(jnp.bfloat16))
    return (layout([answer_root]), layout(answer_mid), layout(answer_leaf))
```

```python
from types import SimpleNamespace

import jax
import jax.numpy as jnp
from jax import lax
from jax.experimental import pallas as pl
from jax.experimental.pallas import tpu as pltpu
from jax.sharding import PartitionSpec as P

SEPARATOR = 10240
BLOCK_ROWS = 128


def swapped(value, axis, distance):
    return lax.ppermute(value, axis, [(i, i ^ 1 << distance) for i in range(lax.axis_size(axis))])


def rotate_parts(vec):
    half = vec.shape[1] // 2
    return jnp.concatenate([-vec[:, half:], vec[:, :half]], axis=1)


def complex_apply(matrix, vec):
    first = jnp.dot(matrix[0], vec, preferred_element_type=jnp.float32)
    second = jnp.dot(matrix[1], rotate_parts(vec), preferred_element_type=jnp.float32)
    return first + second


def complex_apply_t(matrix, vec):
    dims = (((0,), (0,)), ((), ()))
    first = lax.dot_general(matrix[0], vec, dims, preferred_element_type=jnp.float32)
    second = lax.dot_general(matrix[1], rotate_parts(vec), dims, preferred_element_type=jnp.float32)
    return first + second


def bit_set(cube_at, bit):
    return cube_at >> bit & 1 == 1


def gather_bits(piece, count, cube_at):
    for bit in range(count):
        other = swapped(piece, "cube", bit)
        upper = bit_set(cube_at, bit)
        piece = jnp.where(
            upper, jnp.concatenate([other, piece], 0), jnp.concatenate([piece, other], 0)
        )
    return piece


def swap_sum(value, bit):
    return swapped(value.astype(jnp.bfloat16), "cube", bit).astype(value.dtype)


def halve_bits(total, count, cube_at):
    for bit in reversed(range(count)):
        rows = total.shape[0] // 2
        lower = total[:rows]
        higher = total[rows:]
        upper = bit_set(cube_at, bit)
        sent = jnp.where(upper, lower, higher)
        kept = jnp.where(upper, higher, lower)
        total = kept + swap_sum(sent, bit)
    return total


def blk_total(value):
    return lax.psum(value, "blk")


def row_mask(start, count, limit):
    rows = start + jnp.arange(count, dtype=jnp.int32)
    return (rows < limit).astype(jnp.float32)[:, None]


def extend_add(gathered, targets, first_block, slice_blocks):
    blocks = gathered.reshape(targets.shape[0], BLOCK_ROWS, gathered.shape[1])
    slots = jnp.arange(slice_blocks, dtype=jnp.int32)
    placing = (targets[None, :] - first_block == slots[:, None]).astype(jnp.bfloat16)
    summed = jnp.einsum("ti,ird->trd", placing, blocks, preferred_element_type=jnp.float32)
    return summed.reshape(slice_blocks * BLOCK_ROWS, gathered.shape[1])


def pick_rows(parent_slice, targets, rows, first_row):
    block_of = rows // BLOCK_ROWS
    table = (block_of[:, None] == jnp.arange(targets.shape[0], dtype=jnp.int32)[None, :]).astype(
        jnp.int32
    )
    target_block = jnp.sum(table * targets[None, :], axis=1)
    where_row = target_block * BLOCK_ROWS + rows % BLOCK_ROWS - first_row
    inside = (where_row >= 0) & (where_row < parent_slice.shape[0])
    values = parent_slice[jnp.clip(where_row, 0, parent_slice.shape[0] - 1)].astype(jnp.float32)
    return jnp.where(inside[:, None], values, 0.0)


def forward_front(pivot, coupling, gathered, column_mask, solved_mask):
    masked = (column_mask * gathered).astype(jnp.bfloat16)
    own_rows = pivot.shape[1]
    if coupling is None:
        sums = blk_total(complex_apply(pivot, masked))
        return ((solved_mask * sums).astype(jnp.bfloat16), None)
    both = jnp.concatenate([complex_apply(pivot, masked), complex_apply(coupling, masked)], 0)
    sums = blk_total(both)
    solved = (solved_mask * sums[:own_rows]).astype(jnp.bfloat16)
    return (solved, sums[own_rows:].astype(jnp.bfloat16))


def per_device_plain(
    rhs_root,
    rhs_mid,
    rhs_leaf,
    pivot_root,
    pivot_mid,
    pivot_leaf,
    coupling_mid,
    coupling_leaf,
    front_blocks,
    child_map,
):
    cube_n = lax.axis_size("cube")
    blk_n = lax.axis_size("blk")
    cube_at = lax.axis_index("cube")
    blk_at = lax.axis_index("blk")
    slice_rows = SEPARATOR // blk_n
    slice_blocks = slice_rows // BLOCK_ROWS
    first_row = blk_at * slice_rows
    first_block = blk_at * slice_blocks
    group_mid = cube_n // 2
    group_leaf = cube_n // 4
    bits_root = cube_n.bit_length() - 1
    bits_mid = bits_root - 1
    bits_leaf = bits_root - 2
    front_mid = cube_at // group_mid
    place_mid = cube_at % group_mid
    front_leaf = cube_at // group_leaf
    place_leaf = cube_at % group_leaf
    size_root = front_blocks[0] * BLOCK_ROWS
    size_mid = front_blocks[1 + front_mid] * BLOCK_ROWS
    size_leaf = front_blocks[3 + front_leaf] * BLOCK_ROWS
    column_leaf = row_mask(first_row, slice_rows, size_leaf)
    column_mid = row_mask(first_row, slice_rows, size_mid)
    column_root = row_mask(first_row, slice_rows, size_root)
    own_leaf = pivot_leaf.shape[1]
    gathered = lax.dynamic_index_in_dim(rhs_leaf, front_leaf, 0, keepdims=False).astype(jnp.float32)
    solved_leaf, update_leaf = forward_front(
        pivot_leaf,
        coupling_leaf,
        gathered,
        column_leaf,
        row_mask(place_leaf * own_leaf, own_leaf, size_leaf),
    )
    own_mid = pivot_mid.shape[1]
    arrived = gather_bits(update_leaf, bits_mid, cube_at)
    targets = lax.dynamic_slice_in_dim(child_map, 2 + 2 * front_mid, 2, 0).reshape(-1)
    gathered = lax.dynamic_index_in_dim(rhs_mid, front_mid, 0, keepdims=False).astype(jnp.float32)
    gathered = gathered - extend_add(arrived, targets, first_block, slice_blocks)
    solved_mid, update_mid = forward_front(
        pivot_mid,
        coupling_mid,
        gathered,
        column_mid,
        row_mask(place_mid * own_mid, own_mid, size_mid),
    )
    own_root = pivot_root.shape[1]
    arrived = gather_bits(update_mid, bits_root, cube_at)
    targets = child_map[0:2].reshape(-1)
    gathered = rhs_root[0].astype(jnp.float32) - extend_add(
        arrived, targets, first_block, slice_blocks
    )
    solved_root, unused = forward_front(
        pivot_root, None, gathered, column_root, row_mask(cube_at * own_root, own_root, size_root)
    )
    total = lax.psum(complex_apply_t(pivot_root, solved_root), "cube")
    full_root = (column_root * total).astype(jnp.bfloat16)
    piece_root = slice_rows // cube_n
    answer_root = lax.dynamic_slice_in_dim(full_root, cube_at * piece_root, piece_root, 0)
    update_rows_mid = coupling_mid.shape[1]
    rows = place_mid * update_rows_mid + jnp.arange(update_rows_mid, dtype=jnp.int32)
    targets = lax.dynamic_slice_in_dim(child_map, front_mid, 1, 0).reshape(-1)
    pulled = blk_total(pick_rows(full_root, targets, rows, first_row)).astype(jnp.bfloat16)
    term = complex_apply_t(pivot_mid, solved_mid) - complex_apply_t(coupling_mid, pulled)
    piece_mid = slice_rows // group_mid
    share = halve_bits(term, bits_mid, cube_at)
    answer_mid = (row_mask(first_row + place_mid * piece_mid, piece_mid, size_mid) * share).astype(
        jnp.bfloat16
    )
    full_mid = gather_bits(answer_mid, bits_mid, cube_at)
    update_rows_leaf = coupling_leaf.shape[1]
    rows = place_leaf * update_rows_leaf + jnp.arange(update_rows_leaf, dtype=jnp.int32)
    targets = lax.dynamic_slice_in_dim(child_map, 2 + front_leaf, 1, 0).reshape(-1)
    pulled = blk_total(pick_rows(full_mid, targets, rows, first_row)).astype(jnp.bfloat16)
    term = complex_apply_t(pivot_leaf, solved_leaf) - complex_apply_t(coupling_leaf, pulled)
    piece_leaf = slice_rows // group_leaf
    share = halve_bits(term, bits_leaf, cube_at)
    answer_leaf = (
        row_mask(first_row + place_leaf * piece_leaf, piece_leaf, size_leaf) * share
    ).astype(jnp.bfloat16)
    return (answer_root[None], answer_mid[None], answer_leaf[None])

MESH = pl.DeviceIdType.MESH
VMEM = pltpu.VMEM
BF16 = jnp.bfloat16
F32 = jnp.float32
TILE_ROWS = 256
SLOTS = 6
LANES = 128
WINDOWS = SimpleNamespace(
    reduce_leaf=4,
    gather_leaf=6,
    share_leaf=1,
    reduce_mid=4,
    gather_mid=9,
    share_mid=2,
    sum_mid=4,
    solve_root=4,
    pick_root=1,
    scatter_root=8,
    share_root=5,
    pick_mid=1,
    scatter_mid=5,
    share_mid_t=4,
)
LEAF_FIRST = 9


def f32(value):
    return value.astype(F32)


def bf16(value):
    return value.astype(BF16)


def wait_all(copies):
    for copy in copies:
        copy.wait()


def rotate_rows(value):
    half = value.shape[1] // 2
    sign = jnp.where(lax.broadcasted_iota(jnp.int32, value.shape, 1) < half, -1.0, 1.0)
    return pltpu.roll(value, half, 1) * sign


def live_scale(condition):
    return jnp.where(condition, 1.0, 0.0).astype(F32)


class Links:
    def __init__(self, cube_n, blk_n, send, recv):
        self.cube_n = cube_n
        self.blk_n = blk_n
        self.cube = lax.axis_index("cube")
        self.blk = lax.axis_index("blk")
        self.core = lax.rem(self.blk, 2)
        self.chip = self.blk // 2
        self.used = 0
        self.send = send
        self.recv = recv

    def start(self, src, dst, device):
        at = self.used
        self.used += 1
        copy = pltpu.make_async_remote_copy(
            src_ref=src,
            dst_ref=dst,
            send_sem=self.send.at[at],
            recv_sem=self.recv.at[at],
            device_id=device,
            device_id_type=MESH,
        )
        copy.start()
        return copy

    def sibling(self):
        return (self.cube, self.chip * 2 + 1 - self.core)

    def across(self):
        return (self.cube, (1 - self.chip) * 2 + self.core)

    def blk_peer(self, step):
        other = lax.rem(self.blk + step, self.blk_n)
        return other, (self.cube, other)

    def chip_steps(self, group):
        steps = [(s, t) for s in range(group) for t in range(2) if s or t]
        return sorted(steps, key=lambda st: bin(st[0]).count("1") + st[1])

    def chip_peer(self, group, step, back=False):
        place = lax.rem(self.cube, group)
        ahead = group - step[0] if back else step[0]
        other = lax.rem(place + ahead, group)
        chip = lax.rem(self.chip + step[1], 2)
        return other, chip, (self.cube - place + other, chip * 2 + self.core)

    def barrier_signal(self):
        barrier = pltpu.get_barrier_semaphore()
        peers = [self.chip_peer(self.cube_n, s)[2] for s in self.chip_steps(self.cube_n)]
        peers.append(self.sibling())
        peers.append((self.cube, (1 - self.chip) * 2 + 1 - self.core))
        for peer in peers:
            pl.semaphore_signal(barrier, inc=1, device_id=peer, device_id_type=MESH)
        return barrier, len(peers)


def sum_chain(links, src, got_core, half, got_chip, dst):
    core = links.core
    copy = links.start(src.at[1 - core], got_core, links.sibling())
    yield
    copy.wait()
    half[...] = bf16(f32(src[core]) + f32(got_core[...]))
    copy = links.start(half, got_chip, links.across())
    yield
    copy.wait()
    dst[core] = bf16(f32(half[...]) + f32(got_chip[...]))
    copy = links.start(dst.at[core], dst.at[core], links.sibling())
    yield
    copy.wait()


def advance(chain):
    next(chain, None)


class Bulk:
    def __init__(self, ring, sems, segments):
        self.ring = ring
        self.sems = sems
        self.segments = []
        start = 0
        for ref, first, count, body in segments:
            self.segments.append((start, start + count, ref, first, body))
            start += count
        self.total = start
        self.at = 0

    def segment(self, at):
        for segment in self.segments:
            if segment[0] <= at < segment[1]:
                return segment
        return None

    def tile(self, segment, i):
        start, _, ref, first, _ = segment
        slot = lax.rem(jnp.int32(i), SLOTS)
        row = pl.multiple_of((i - start + first) * TILE_ROWS, TILE_ROWS)
        return pltpu.make_async_copy(
            ref.at[:, pl.ds(row, TILE_ROWS), :], self.ring.at[slot], self.sems.at[slot]
        )

    def prime(self):
        for i in range(min(SLOTS - 1, self.total)):
            self.tile(self.segment(i), jnp.int32(i)).start()

    def run(self, count):
        end = min(self.at + count, self.total)
        while self.at < end:
            now = self.segment(self.at)
            later = self.segment(self.at + SLOTS - 1)
            stop = min(end, now[1])
            if later is not None:
                stop = min(stop, later[1] - SLOTS + 1)

            def step(i, now=now, later=later):
                if later is not None:
                    self.tile(later, i + SLOTS - 1).start()
                self.tile(now, i).wait()
                now[4](i - now[0] + now[3], self.ring.at[lax.rem(i, SLOTS)])

            pl.loop(self.at, stop)(step)
            self.at = stop


def per_device_fast(
    rhs_root,
    rhs_mid,
    rhs_leaf,
    pivot_root,
    pivot_mid,
    pivot_leaf,
    coupling_mid,
    coupling_leaf,
    front_blocks,
    child_map,
):
    cube_n = lax.axis_size("cube")
    blk_n = lax.axis_size("blk")
    width = pivot_root.shape[2]
    blocks = width // BLOCK_ROWS
    own_leaf = pivot_leaf.shape[1]
    own_mid = pivot_mid.shape[1]
    own_root = pivot_root.shape[1]
    up_leaf = coupling_leaf.shape[1]
    up_mid = coupling_mid.shape[1]
    shard_leaf = up_leaf // blk_n
    shard_mid = up_mid // blk_n
    group_root = cube_n
    group_mid = cube_n // 2
    group_leaf = cube_n // 4
    rows_mid = group_mid * up_leaf
    rows_root = group_root * up_mid
    child_blocks = child_map.shape[1]
    n_up = 2 * child_blocks
    tiles_leaf = own_leaf // TILE_ROWS
    tiles_mid = own_mid // TILE_ROWS
    tiles_root = own_root // TILE_ROWS
    half_leaf = own_leaf // 4
    half_mid = own_mid // 2
    piece_root = width // group_root
    piece_mid = width // group_mid
    piece_leaf = width // group_leaf
    pairs_root = group_root // 2
    pairs_mid = group_mid // 2

    def vm(*shape):
        return VMEM(shape + (LANES,), BF16)

    n_copies = 160
    names = dict(
        send=pltpu.SemaphoreType.DMA((n_copies,)),
        recv=pltpu.SemaphoreType.DMA((n_copies,)),
        ring_sem=pltpu.SemaphoreType.DMA((SLOTS,)),
        load_sem=pltpu.SemaphoreType.DMA((10,)),
        ring=VMEM((SLOTS, 2, TILE_ROWS, width), BF16),
        leaf_c=VMEM((2, up_leaf, width), BF16),
        mid_c=VMEM((2, up_mid, width), BF16),
        root_a=VMEM((2, own_root, width), BF16),
        r_leaf=vm(blocks, BLOCK_ROWS),
        r_mid=vm(blocks, BLOCK_ROWS),
        r_root=vm(blocks, BLOCK_ROWS),
        x_blocks=vm(blocks, BLOCK_ROWS),
        v_leaf=vm(2, width),
        v_mid=vm(2, width),
        v_root=vm(2, width),
        part1=vm(up_leaf),
        got1=vm(blk_n - 1, shard_leaf),
        own1=vm(shard_leaf),
        up1=vm(rows_mid),
        part2=vm(up_mid),
        got2=vm(blk_n - 1, shard_mid),
        own2=vm(shard_mid),
        up2=vm(rows_root),
        runs=VMEM((n_up + 1, BLOCK_ROWS, LANES), F32),
        y_leaf=vm(4, half_leaf),
        gc_leaf=vm(2, half_leaf),
        h_leaf=vm(2, half_leaf),
        gx_leaf=vm(2, half_leaf),
        s_leaf=vm(4, half_leaf),
        y_mid=vm(2, half_mid),
        gc_mid=vm(half_mid),
        h_mid=vm(half_mid),
        gx_mid=vm(half_mid),
        s_mid=vm(2, half_mid),
        y_root=vm(tiles_root, 2, TILE_ROWS // 2),
        gc_root=vm(tiles_root, TILE_ROWS // 2),
        h_root=vm(tiles_root, TILE_ROWS // 2),
        gx_root=vm(tiles_root, TILE_ROWS // 2),
        s_root=vm(tiles_root, 2, TILE_ROWS // 2),
        acc_leaf=VMEM((LANES, width), F32),
        acc_mid=VMEM((LANES, width), F32),
        pick1=vm(group_root, 2, 2, shard_mid),
        pick1_core=vm(group_root, 2, shard_mid),
        pick1_sum=vm(group_root, 2, shard_mid),
        pick1_got=vm(2 * group_root - 1, shard_mid),
        pulled1=vm(blk_n, shard_mid),
        pick2=vm(group_mid, 2, 2, shard_leaf),
        pick2_core=vm(group_mid, 2, shard_leaf),
        pick2_sum=vm(group_mid, 2, shard_leaf),
        pick2_got=vm(2 * group_mid - 1, shard_leaf),
        pulled2=vm(blk_n, shard_leaf),
        pair_root=vm(pairs_root, piece_root),
        psum_root=vm(pairs_root, piece_root),
        rest_root=vm(pairs_root - 1, piece_root),
        pair_mid=vm(pairs_mid, piece_mid),
        psum_mid=vm(pairs_mid, piece_mid),
        rest_mid=vm(max(pairs_mid - 1, 1), piece_mid),
        got_leaf=vm(group_leaf - 1, piece_leaf),
        prev=pltpu.SMEM((2, n_up), jnp.int32),
        last=pltpu.SMEM((2, blocks), jnp.int32),
    )
    keys = list(names)

    def kernel(*refs):
        (g_root, g_mid, g_leaf, p_root, p_mid, p_leaf, c_mid, c_leaf, fronts, cmap) = refs[:10]
        out_root, out_mid, out_leaf = refs[10:13]
        m = SimpleNamespace(**dict(zip(keys, refs[13:])))
        links = Links(cube_n, blk_n, m.send, m.recv)
        cube, blk, core, chip = links.cube, links.blk, links.core, links.chip
        first_block = blk * blocks
        place_mid = lax.rem(cube, group_mid)
        front_mid = cube // group_mid
        place_leaf = lax.rem(cube, group_leaf)
        front_leaf = cube // group_leaf
        live_root = fronts[0]
        live_mid = fronts[1 + front_mid]
        live_leaf = fronts[3 + front_leaf]

        def load(src, dst, at):
            copy = pltpu.make_async_copy(src, dst, m.load_sem.at[at])
            copy.start()
            return copy

        def apply_rows(matrix, rows, v_ref):
            total = jnp.dot(matrix[0, rows], v_ref[0], preferred_element_type=F32)
            return total + jnp.dot(matrix[1, rows], v_ref[1], preferred_element_type=F32)

        def forward_body(y_ref, v_ref):
            per = y_ref.shape[1] // TILE_ROWS

            def body(j, tile):
                total = jnp.dot(tile[0], v_ref[0], preferred_element_type=F32)
                total += jnp.dot(tile[1], v_ref[1], preferred_element_type=F32)
                at = pl.ds(pl.multiple_of(lax.rem(j, per) * TILE_ROWS, TILE_ROWS), TILE_ROWS)
                y_ref[j // per, at, :] = bf16(total)

            return body

        def columns_of(value, block, live):
            parts = []
            for n in range(TILE_ROWS // BLOCK_ROWS):
                piece = f32(value[n * BLOCK_ROWS : (n + 1) * BLOCK_ROWS])
                parts.append((piece * live_scale(block + n < live)).T)
            whole = jnp.concatenate(parts, axis=1)
            half = LANES // 2
            turned = jnp.concatenate([-whole[half:], whole[:half]], axis=0)
            return bf16(whole), bf16(turned)

        def transposed_body(s_ref, acc, block0, live):
            per = s_ref.shape[1] // TILE_ROWS

            def body(j, tile):
                at = pl.ds(pl.multiple_of(lax.rem(j, per) * TILE_ROWS, TILE_ROWS), TILE_ROWS)
                block = block0 + j * (TILE_ROWS // BLOCK_ROWS)
                pair = columns_of(s_ref[j // per, at, :], block, live)
                vec = jnp.concatenate(pair, axis=1)
                both = tile[...].reshape(2 * TILE_ROWS, width)
                acc[...] += jnp.dot(vec, both, preferred_element_type=F32)

            return body

        leaf_t = transposed_body(
            m.s_leaf, m.acc_leaf, place_leaf * (own_leaf // BLOCK_ROWS), live_leaf
        )
        mid_t = transposed_body(
            m.s_mid, m.acc_mid, place_mid * (own_mid // BLOCK_ROWS), live_mid
        )
        bulk = Bulk(
            m.ring,
            m.ring_sem,
            [
                (p_leaf, 0, tiles_leaf, forward_body(m.y_leaf, m.v_leaf)),
                (p_mid, 0, tiles_mid, forward_body(m.y_mid, m.v_mid)),
                (p_leaf, 0, LEAF_FIRST, leaf_t),
                (p_mid, 0, tiles_mid, mid_t),
                (p_leaf, LEAF_FIRST, tiles_leaf - LEAF_FIRST, leaf_t),
            ],
        )

        def chart(level, row):
            targets = [
                cmap[row + i // child_blocks, i % child_blocks] - first_block for i in range(n_up)
            ]
            for i in range(n_up):
                found = jnp.int32(0)
                for j in range(i):
                    found = jnp.where(targets[j] == targets[i], j + 1, found)
                m.prev[level, i] = found

            @pl.loop(0, blocks)
            def _(t):
                found = jnp.int32(0)
                for i in range(n_up):
                    found = jnp.where(targets[i] == t, i + 1, found)
                m.last[level, t] = found

        def write_vector(v_ref, t, value, live):
            value = value * live_scale(first_block + t < live)
            at = pl.ds(pl.multiple_of(t * BLOCK_ROWS, BLOCK_ROWS), BLOCK_ROWS)
            v_ref[0, at, :] = bf16(value)
            v_ref[1, at, :] = bf16(rotate_rows(value))

        def gathered(level, up_ref, rhs_ref, v_ref, live):
            runs = m.runs

            @pl.loop(0, n_up)
            def _(i):
                at = pl.ds(pl.multiple_of(i * BLOCK_ROWS, BLOCK_ROWS), BLOCK_ROWS)
                runs[i + 1] = f32(up_ref[at, :]) + runs[m.prev[level, i]]

            @pl.loop(0, blocks)
            def _(t):
                value = f32(rhs_ref[t]) - runs[m.last[level, t]]
                write_vector(v_ref, t, value, live)

        def reduce_start(matrix, v_ref, part, got, shard, ready):
            copies = []
            for k in range(1, blk_n + 1):
                other, device = links.blk_peer(k)
                at = pl.ds(pl.multiple_of(other * shard, 16), shard)
                if k in ready:
                    ready[k]()
                part[at, :] = bf16(apply_rows(matrix, at, v_ref))
                if k < blk_n:
                    copies.append(links.start(part.at[at], got.at[k - 1], device))
            return copies

        def reduce_end(copies, part, got, own, up, shard, group):
            wait_all(copies)
            at = pl.ds(pl.multiple_of(blk * shard, 16), shard)
            total = f32(part[at, :])
            for k in range(1, blk_n):
                total = total + f32(got[k - 1])
            own[...] = bf16(total)
            place = lax.rem(cube, group)

            def spot(cube_at, chip_at):
                row = ((cube_at * 2 + chip_at) * 2 + core) * shard
                return up.at[pl.ds(pl.multiple_of(row, 16), shard)]

            mine = pl.ds(pl.multiple_of(((place * 2 + chip) * 2 + core) * shard, 16), shard)
            up[mine, :] = own[...]
            far = []
            for step in links.chip_steps(group):
                _, _, device = links.chip_peer(group, step)
                far.append((step, links.start(own, spot(place, chip), device)))
            near = [links.start(own, spot(place, chip), links.sibling())]
            return far, near, spot

        def share(far, near, spot, group):
            for step, copy in far:
                copy.wait()
                other, chip_at, _ = links.chip_peer(group, step, back=True)
                where = spot(other, chip_at)
                near.append(links.start(where, where, links.sibling()))

        def pick(row, picks, shard):
            per_core = shard
            for i in range(n_up):
                target = cmap[row + i // child_blocks, i % child_blocks] - first_block
                inside = jnp.logical_and(target >= 0, target < blocks)
                block = f32(m.x_blocks[jnp.clip(target, 0, blocks - 1)])
                block = bf16(block * live_scale(inside))
                done = 0
                while done < BLOCK_ROWS:
                    line = i * BLOCK_ROWS + done
                    piece, offset = line // per_core, line % per_core
                    count = min(per_core - offset, BLOCK_ROWS - done)
                    picks[piece // 4, piece // 2 % 2, piece % 2, offset : offset + count, :] = block[
                        done : done + count
                    ]
                    done += count

        def pick_core(picks, got):
            return links.start(picks.at[:, :, 1 - core], got, links.sibling())

        def pick_scatter(copy, picks, got_core, total, got, group):
            copy.wait()
            total[...] = bf16(f32(picks[:, :, core]) + f32(got_core[...]))
            copies = []
            for n, step in enumerate(links.chip_steps(group)):
                other, chip_at, device = links.chip_peer(group, step)
                copies.append(links.start(total.at[other, chip_at], got.at[n], device))
            return copies

        def pick_share(copies, total, got, pulled, group):
            value = f32(total[lax.rem(cube, group), chip])
            for n, copy in enumerate(copies):
                copy.wait()
                value = value + f32(got[n])
            pulled[blk] = bf16(value)
            mine = pulled.at[blk]
            out = []
            for k in range(1, blk_n):
                out.append(links.start(mine, mine, links.blk_peer(k)[1]))
            return out

        def pulled_term(matrix, pulled, rows):
            value = pulled[...].reshape(rows, LANES)
            turned = bf16(rotate_rows(f32(value)))
            dims = (((0,), (0,)), ((), ()))
            total = lax.dot_general(value, matrix[0], dims, preferred_element_type=F32)
            return total + lax.dot_general(turned, matrix[1], dims, preferred_element_type=F32)

        def to_rows(acc, x_ref, live):
            @pl.loop(0, blocks)
            def _(t):
                at = pl.ds(pl.multiple_of(t * BLOCK_ROWS, BLOCK_ROWS), BLOCK_ROWS)
                value = acc[:, at].T * live_scale(first_block + t < live)
                x_ref[at, :] = bf16(value)
                m.x_blocks[t] = bf16(value)

        def pair_device():
            return (cube + 1 - 2 * lax.rem(cube, 2), blk)

        def pair_start(x_ref, got, pairs, piece):
            side = 1 - lax.rem(cube, 2)
            copies = []
            for n in range(pairs):
                row = pl.multiple_of((2 * n + side) * piece, 16)
                copies.append(links.start(x_ref.at[pl.ds(row, piece)], got.at[n], pair_device()))
            return copies

        def pair_end(copies, x_ref, got, total, rest, pairs, piece):
            wait_all(copies)
            side = lax.rem(cube, 2)
            for n in range(pairs):
                row = pl.multiple_of((2 * n + side) * piece, 16)
                total[n] = bf16(f32(x_ref[pl.ds(row, piece), :]) + f32(got[n]))
            out = []
            place = lax.rem(cube // 2, pairs)
            base = cube // 2 - place
            for k in range(1, pairs):
                other = lax.rem(place + k, pairs)
                device = ((base + other) * 2 + side, blk)
                out.append(links.start(total.at[other], rest.at[k - 1], device))
            return out

        def rest_end(copies, total, rest, out, pairs):
            value = f32(total[lax.rem(cube // 2, pairs)])
            for n, copy in enumerate(copies):
                copy.wait()
                value = value + f32(rest[n])
            out[...] = bf16(value)

        load_rhs = load(g_leaf.at[front_leaf], m.r_leaf, 0)
        load_c = []
        for k in range(1, blk_n + 1):
            other, _ = links.blk_peer(k)
            at = pl.ds(pl.multiple_of(other * shard_leaf, 16), shard_leaf)
            load_c.append(load(c_leaf.at[:, at, :], m.leaf_c.at[:, at, :], k))
        barrier, arrivals = links.barrier_signal()
        m.runs[0] = jnp.zeros((BLOCK_ROWS, LANES), F32)
        m.acc_leaf[...] = jnp.zeros((LANES, width), F32)
        m.acc_mid[...] = jnp.zeros((LANES, width), F32)
        load_rhs.wait()

        @pl.loop(0, blocks)
        def _(t):
            write_vector(m.v_leaf, t, f32(m.r_leaf[t]), live_leaf)

        pl.semaphore_wait(barrier, arrivals)
        ready = {k: load_c[k - 1].wait for k in range(1, blk_n + 1)}
        copies = reduce_start(
            m.leaf_c, m.v_leaf, m.part1, m.got1, shard_leaf, ready
        )
        bulk.prime()
        load_mid = load(g_mid.at[front_mid], m.r_mid, 5)
        load_cm = load(c_mid, m.mid_c, 6)
        chart(0, 2 + 2 * front_mid)
        bulk.run(WINDOWS.reduce_leaf)
        moves = reduce_end(
            copies, m.part1, m.got1, m.own1, m.up1, shard_leaf, group_mid
        )
        bulk.run(WINDOWS.gather_leaf)
        share(*moves, group_mid)
        load_root = load(g_root.at[0], m.r_root, 7)
        load_a = load(p_root, m.root_a, 8)
        sum_a = sum_chain(
            links,
            m.y_leaf.at[0:2],
            m.gc_leaf.at[0],
            m.h_leaf.at[0],
            m.gx_leaf.at[0],
            m.s_leaf.at[0:2],
        )
        sum_b = sum_chain(
            links,
            m.y_leaf.at[2:4],
            m.gc_leaf.at[1],
            m.h_leaf.at[1],
            m.gx_leaf.at[1],
            m.s_leaf.at[2:4],
        )
        assert bulk.at * 2 >= tiles_leaf
        advance(sum_a)
        bulk.run(WINDOWS.share_leaf)
        wait_all(moves[1])
        load_mid.wait()
        gathered(0, m.up1, m.r_mid, m.v_mid, live_mid)
        load_cm.wait()
        copies = reduce_start(m.mid_c, m.v_mid, m.part2, m.got2, shard_mid, {})
        advance(sum_a)
        chart(1, 0)
        bulk.run(WINDOWS.reduce_mid)
        moves = reduce_end(
            copies, m.part2, m.got2, m.own2, m.up2, shard_mid, group_root
        )
        bulk.run(tiles_leaf - bulk.at)
        advance(sum_a)
        advance(sum_b)
        bulk.run(WINDOWS.gather_mid - 5)
        advance(sum_b)
        bulk.run(4)
        share(*moves, group_root)
        bulk.run(tiles_leaf + tiles_mid - bulk.at)
        sum_c = sum_chain(
            links, m.y_mid, m.gc_mid, m.h_mid, m.gx_mid, m.s_mid
        )
        advance(sum_c)
        wait_all(moves[1])
        load_root.wait()
        gathered(1, m.up2, m.r_root, m.v_root, live_root)
        load_a.wait()
        advance(sum_a)
        advance(sum_b)

        chains = []
        for n in range(tiles_root):
            at = pl.ds(n * TILE_ROWS, TILE_ROWS)
            total = apply_rows(m.root_a, at, m.v_root)
            m.y_root[n] = bf16(total).reshape(2, TILE_ROWS // 2, LANES)
            chains.append(
                sum_chain(
                    links,
                    m.y_root.at[n],
                    m.gc_root.at[n],
                    m.h_root.at[n],
                    m.gx_root.at[n],
                    m.s_root.at[n],
                )
            )
            advance(chains[n])
            if n:
                advance(chains[n - 1])
        advance(sum_b)
        bulk.run(1)
        advance(chains[-1])
        advance(sum_c)
        bulk.run(WINDOWS.solve_root - 1)
        for chain in chains:
            advance(chain)
        block0 = cube * (own_root // BLOCK_ROWS)
        for n in range(tiles_root):
            advance(chains[n])
            value = m.s_root[n].reshape(TILE_ROWS, LANES)
            block = block0 + n * (TILE_ROWS // BLOCK_ROWS)
            whole, turned = columns_of(value, block, live_root)
            at = pl.ds(n * TILE_ROWS, TILE_ROWS)
            total = jnp.dot(whole, m.root_a[0, at], preferred_element_type=F32)
            total += jnp.dot(turned, m.root_a[1, at], preferred_element_type=F32)
            m.acc_mid[...] += total
        x_root = m.v_leaf.at[0]
        to_rows(m.acc_mid, x_root, live_root)
        m.acc_mid[...] = jnp.zeros((LANES, width), F32)
        pick(0, m.pick1, shard_mid)
        copy = pick_core(m.pick1, m.pick1_core)
        bulk.run(WINDOWS.pick_root)
        copies = pick_scatter(
            copy, m.pick1, m.pick1_core, m.pick1_sum, m.pick1_got, group_root
        )
        advance(sum_c)
        bulk.run(tiles_leaf + tiles_mid + LEAF_FIRST - bulk.at)
        advance(sum_c)
        bulk.run(WINDOWS.scatter_root)
        copies = pick_share(copies, m.pick1_sum, m.pick1_got, m.pulled1, group_root)
        answer_root = pair_start(x_root, m.pair_root, pairs_root, piece_root)
        bulk.run(tiles_leaf + 2 * tiles_mid + LEAF_FIRST - bulk.at)
        wait_all(copies)
        m.acc_mid[...] -= pulled_term(m.mid_c, m.pulled1, up_mid)
        x_mid = m.v_leaf.at[1]
        to_rows(m.acc_mid, x_mid, live_mid)
        pick(2 + 2 * front_mid, m.pick2, shard_leaf)
        copy = pick_core(m.pick2, m.pick2_core)
        bulk.run(WINDOWS.pick_mid)
        copies = pick_scatter(
            copy, m.pick2, m.pick2_core, m.pick2_sum, m.pick2_got, group_mid
        )
        bulk.run(WINDOWS.scatter_mid)
        copies = pick_share(copies, m.pick2_sum, m.pick2_got, m.pulled2, group_mid)
        answer_mid = pair_start(x_mid, m.pair_mid, pairs_mid, piece_mid)
        answer_root = pair_end(
            answer_root,
            x_root,
            m.pair_root,
            m.psum_root,
            m.rest_root,
            pairs_root,
            piece_root,
        )
        bulk.run(bulk.total - bulk.at)
        wait_all(copies)
        m.acc_leaf[...] -= pulled_term(m.leaf_c, m.pulled2, up_leaf)
        x_leaf = m.v_mid.at[0]
        to_rows(m.acc_leaf, x_leaf, live_leaf)
        copies = []
        for k in range(1, group_leaf):
            other = lax.rem(place_leaf + k, group_leaf)
            row = pl.multiple_of(other * piece_leaf, 16)
            device = (cube - place_leaf + other, blk)
            copies.append(links.start(x_leaf.at[pl.ds(row, piece_leaf)], m.got_leaf.at[k - 1], device))
        answer_mid = pair_end(
            answer_mid, x_mid, m.pair_mid, m.psum_mid, m.rest_mid, pairs_mid, piece_mid
        )
        rest_end(answer_root, m.psum_root, m.rest_root, out_root, pairs_root)
        rest_end(answer_mid, m.psum_mid, m.rest_mid, out_mid, pairs_mid)
        wait_all(copies)
        row = pl.multiple_of(place_leaf * piece_leaf, 16)
        value = f32(x_leaf[pl.ds(row, piece_leaf), :])
        for k in range(1, group_leaf):
            value = value + f32(m.got_leaf[k - 1])
        out_leaf[...] = bf16(value)
        assert links.used <= n_copies

    hbm = pl.BlockSpec(memory_space=pl.ANY)
    smem = pl.BlockSpec(memory_space=pltpu.SMEM)
    outs = pl.pallas_call(
        kernel,
        out_shape=[
            jax.ShapeDtypeStruct((piece_root, LANES), BF16),
            jax.ShapeDtypeStruct((piece_mid, LANES), BF16),
            jax.ShapeDtypeStruct((piece_leaf, LANES), BF16),
        ],
        in_specs=[hbm] * 8 + [smem] * 2,
        out_specs=[pl.BlockSpec(memory_space=VMEM)] * 3,
        scratch_shapes=list(names.values()),
        compiler_params=pltpu.CompilerParams(
            collective_id=0, has_side_effects=True, vmem_limit_bytes=64 * 1024 * 1024 - 65536
        ),
    )(
        rhs_root.reshape(-1, blocks, BLOCK_ROWS, LANES),
        rhs_mid.reshape(-1, blocks, BLOCK_ROWS, LANES),
        rhs_leaf.reshape(-1, blocks, BLOCK_ROWS, LANES),
        pivot_root,
        pivot_mid,
        pivot_leaf,
        coupling_mid,
        coupling_leaf,
        front_blocks,
        child_map,
    )
    return tuple(out[None] for out in hand_on(outs))


def hand_on(arrays):
    n = len(arrays)

    def kernel(*refs):
        into, out = refs[3 * n], refs[3 * n + 1]
        first = [pltpu.make_async_copy(refs[i], refs[2 * n + i], into.at[i]) for i in range(n)]
        second = [pltpu.make_async_copy(refs[2 * n + i], refs[n + i], out.at[i]) for i in range(n)]
        for copy in first:
            copy.start()
        for i in range(n):
            first[i].wait()
            second[i].start()
        for copy in second:
            copy.wait()

    hbm = pl.BlockSpec(memory_space=pl.ANY)
    return pl.pallas_call(
        kernel,
        out_shape=[jax.ShapeDtypeStruct(a.shape, a.dtype) for a in arrays],
        in_specs=[hbm] * n,
        out_specs=[hbm] * n,
        scratch_shapes=[VMEM(a.shape, a.dtype) for a in arrays]
        + [pltpu.SemaphoreType.DMA((n,)), pltpu.SemaphoreType.DMA((n,))],
    )(*arrays)


def per_device(*args):
    cube_n = lax.axis_size("cube")
    blk_n = lax.axis_size("blk")
    pivot_root, pivot_mid, pivot_leaf, coupling_mid = args[3], args[4], args[5], args[6]
    fits = (
        blk_n == 4
        and cube_n % 4 == 0
        and args[0].shape[2] == LANES
        and coupling_mid.shape[1] % (16 * blk_n) == 0
        and pivot_root.shape[1] % TILE_ROWS == 0
        and pivot_mid.shape[1] % (2 * TILE_ROWS) == 0
        and pivot_leaf.shape[1] % (4 * TILE_ROWS) == 0
        and pivot_root.shape[2] % (16 * cube_n) == 0
    )
    return per_device_fast(*args) if fits else per_device_plain(*args)


def solution(mesh):
    in_specs = (
        P(None, "blk", None),
        P(None, "blk", None),
        P(None, "blk", None),
        P(None, "cube", "blk"),
        P(None, "cube", "blk"),
        P(None, "cube", "blk"),
        P(None, "cube", "blk"),
        P(None, "cube", "blk"),
        P(),
        P(),
    )
    out_specs = (P("blk", "cube", None), P("blk", "cube", None), P("blk", "cube", None))
    return jax.shard_map(
        per_device, mesh=mesh, in_specs=in_specs, out_specs=out_specs, check_vma=False
    )
```
